32 devices in a mesh: samp: 16 (over z, y, x), tm: 2 (over core).
Axes of the slice: x: 2, y: 2, z: 4, core: 2. Of those that a mesh axis runs over, the one named last changes fastest.
Arguments:
- sources: bfloat16 [256, 128, 1024], P('samp', 'tm'), may hold values from -6 to 6
- operator: bfloat16 [16, 1024, 128], P(None, 'samp'), may hold values from -0.046875 to 0.046875
- lag_order: int32 [16], replicated, may hold values from 0 to 15, each once
Outputs:
- records: bfloat16 [256, 128, 128], P('samp', 'tm')
The draws below stay inside these ranges and needn't reach their ends.
Inputs may be any that keep to these rules, and one draw needn't show every extreme that they name: `lag_order`: each lag 0 to 15 stands in exactly one slot.
All inputs are finite; a program needn't handle non-finite values.
Results may differ from the reference program's by a relative error of at most 0.001.
Values may be sent and summed in bfloat16 or wider, within the bound.
A program may use at most 64 MiB of HBM per device.

```python
import jax
import jax.numpy as jnp
from jax import lax

S = 128
J = 1024
LAGS = 16
SAMPLES = 256
TIMES = 128


def shard_levels(rng, shape, cuts, low, largest):
    def one(axis_at, blocks):
        draws = jax.random.uniform(jax.random.fold_in(jax.random.fold_in(rng, 6), axis_at), (blocks,), jnp.float32, low / len(cuts), largest / len(cuts))
        return jnp.repeat(jnp.exp(draws), shape[axis_at] // blocks).reshape((-1,) + (1,) * (len(shape) - axis_at - 1))

    loudness = one(*cuts[0])
    for cut in cuts[1:]:
        loudness = loudness * one(*cut)
    return loudness


def noise(own_key, extent, deviation, bound, split=(), kind=jnp.bfloat16):
    array = deviation * jax.random.normal(own_key, extent, jnp.float32)
    if split:
        array = array * shard_levels(own_key, extent, split, -0.22, 0.18)
    return jnp.clip(array, -bound, bound).astype(kind)


def setup_inputs(seed: int = 0) -> dict:
    streams_of = jax.random.split(jax.random.key(seed), 4)
    sources = noise(streams_of[0], (SAMPLES, TIMES, J), 1.0, 6.0, ((0, 16), (1, 2)))
    operator = noise(streams_of[1], (LAGS, J, S), (LAGS * J) ** -0.5, 0.046875, ((1, 16),))
    lag_order = jax.random.permutation(streams_of[2], LAGS).astype(jnp.int32)
    return dict(sources=sources, operator=operator, lag_order=lag_order)


def reference(sources, operator, lag_order):
    border = LAGS - 1
    padded = jnp.pad(sources, ((0, 0), (border, 0), (0, 0)))
    count = sources.shape[1]

    def step(total, slot):
        lag = lag_order[slot].astype(jnp.int32)
        start = (border - lag).astype(jnp.int32)
        shifted = lax.dynamic_slice_in_dim(padded, start, count, 1).astype(jnp.float32)
        block = operator[slot].astype(jnp.float32)
        return total + jnp.einsum("btj,js->bts", shifted, block), None

    init = jnp.zeros((sources.shape[0], count, operator.shape[2]), jnp.float32)
    total, unused = lax.scan(step, init, jnp.arange(LAGS, dtype=jnp.int32))
    return total.astype(jnp.bfloat16)
```

```python
import functools
import math

import jax
import jax.numpy as jnp
from jax import lax
from jax.experimental import pallas as pl
from jax.experimental.pallas import tpu as pltpu
from jax.sharding import PartitionSpec as P

MESH = pl.DeviceIdType.MESH
HALO = 16
Z, A, B = 0, 1, 2
ORDERS = ((Z, A, B), (B, Z, A))


def when(cond, fn):
    if cond is True:
        fn()
    elif cond is not False:
        pl.when(cond)(fn)


def ranked(me, size, rank):
    if rank == 0:
        return me, None
    if size == 2:
        return 1 - me, None
    low = jnp.minimum(me, size - 1 - me)
    side = 1 - 2 * (me // ((size + 1) // 2))
    alternate = (rank + 1) // 2 if rank % 2 else -((rank + 1) // 2)
    near = rank <= 2 * low
    offset = side * jnp.where(near, alternate, rank - low)
    away = side * jnp.where(near, -1 if rank % 2 else 1, -1)
    return me + offset, away


def fused(sizes, n_tm, lags, src_hbm, op_ref, lag_ref, out_ref,
          xin, halo, xt, w, acc, in_sem, halo_send, halo_recv, send_sem, recv_sem):
    planes, side_size, _ = sizes
    batch, window, _ = xin.shape
    depth = op_ref.shape[1]
    sensors = op_ref.shape[2]
    pairs = lags // 2
    piece = pairs // 4
    width = side_size * side_size * depth
    samp = lax.axis_index("samp")
    tm = lax.axis_index("tm")
    core = tm % 2
    sibling = tm + 1 - 2 * core
    z = samp // (side_size * side_size)
    y = (samp // side_size) % side_size
    x = samp % side_size
    a = x + core * (y - x)
    b = y + core * (x - y)
    stride_a = 1 + core * (side_size - 1)
    stride_b = side_size - core * (side_size - 1)
    me = (z, a, b)

    def flat(at):
        return at[Z] * (side_size * side_size) + at[A] * stride_a + at[B] * stride_b

    def both(d):
        if sizes[d] == 1:
            return []
        if sizes[d] == 2:
            return [(True, 1 - me[d])]
        return [(me[d] > 0, me[d] - 1), (me[d] < sizes[d] - 1, me[d] + 1)]

    def moved(d, to):
        at = list(me)
        at[d] = to
        return flat(at)

    load = pltpu.make_async_copy(src_hbm, xin, in_sem)
    load.start()

    barrier = pltpu.get_barrier_semaphore()
    expected = 1
    pl.semaphore_signal(barrier, inc=1, device_id=(samp, sibling), device_id_type=MESH)
    for d in (Z, A, B):
        for cond, to in both(d):
            when(cond, lambda d=d, to=to: pl.semaphore_signal(
                barrier, inc=1, device_id=(moved(d, to), tm), device_id_type=MESH))
            expected = expected + (1 if cond is True else cond.astype(jnp.int32))
    for cond, to in ((tm > 0, tm - 1), (tm < n_tm - 1, tm + 1)):
        when(cond, lambda to=to: pl.semaphore_signal(
            barrier, inc=1, device_id=(samp, to), device_id_type=MESH))
        expected = expected + cond.astype(jnp.int32)

    own_rows = pl.multiple_of((samp % (side_size * side_size)) * depth, depth)
    for lag in range(lags):
        slot = jnp.int32(0)
        for k in range(lags):
            slot = jnp.where(lag_ref[k] == lag, k, slot)
        w[z, lag // 2, pl.ds(own_rows, depth), (lag % 2) * sensors:(lag % 2 + 1) * sensors] = op_ref[slot]

    pl.semaphore_wait(barrier, expected)

    def block(at, q, of_core):
        rows = pl.multiple_of((flat(at) - at[Z] * (side_size * side_size)) * depth, depth)
        return w.at[at[Z], pl.ds((2 * of_core + q) * piece, piece), pl.ds(rows, depth), :]

    def copy(at, q, slot, device):
        ref = block(at, q, core)
        source = flat(at)
        return pltpu.make_async_remote_copy(
            src_ref=ref, dst_ref=ref,
            send_sem=send_sem.at[q, slot, source],
            recv_sem=recv_sem.at[1 if slot == 6 else 0, q, source],
            device_id=device, device_id_type=MESH)

    sends = []

    def send(cond, at, q, slot, device):
        when(cond, lambda: copy(at, q, slot, device).start())
        sends.append((cond, at, q, slot, device))

    def await_block(at, q, slot):
        copy(at, q, slot, (samp, sibling)).wait_recv()

    def sibling_wait(at, q):
        ref = block(at, q, 1 - core)
        pltpu.make_async_remote_copy(
            src_ref=ref, dst_ref=ref,
            send_sem=send_sem.at[q, 6, flat(at)],
            recv_sem=recv_sem.at[1, q, flat(at)],
            device_id=(samp, sibling), device_id_type=MESH).wait_recv()

    def process(ranks, q):
        order = ORDERS[q]
        spots = [ranked(me[d], sizes[d], ranks[d]) for d in (Z, A, B)]
        at = tuple(s[0] for s in spots)
        last = -1
        for i, d in enumerate(order):
            if ranks[d]:
                last = i
        if last >= 0:
            await_block(at, q, 0)
            d = order[last]
            away = spots[d][1]
            if away is not None:
                to = me[d] + away
                send((to >= 0) & (to < sizes[d]), at, q, 2 * d, (moved(d, to), tm))
        for d in order[last + 1:]:
            for i, (cond, to) in enumerate(both(d)):
                send(cond, at, q, 2 * d + i, (moved(d, to), tm))
        if last >= 0:
            send(True, at, q, 6, (samp, sibling))

    flips = [(i, j) for i in range(side_size) for j in range(side_size)]
    flips.sort(key=sum)

    for q in range(2):
        process((0, 0, 0), q)

    tail = pltpu.make_async_remote_copy(
        src_ref=src_hbm.at[:, pl.ds(window - HALO, HALO), :], dst_ref=halo,
        send_sem=halo_send, recv_sem=halo_recv,
        device_id=(samp, lax.rem(tm + 1, n_tm)), device_id_type=MESH)
    pl.when(tm < n_tm - 1)(tail.start)

    square = batch * HALO
    row = lax.broadcasted_iota(jnp.int32, (square, square), 0)
    col = lax.broadcasted_iota(jnp.int32, (square, square), 1)
    to_time = (col == (row % batch) * HALO + row // batch).astype(jnp.bfloat16)
    to_batch = (col == (row % HALO) * batch + row // HALO).astype(jnp.bfloat16)

    def turn(values, first):
        values = values.reshape(square, values.shape[-1])
        for p in range(planes):
            part = jnp.dot(to_time, values[:, p * width:(p + 1) * width],
                           preferred_element_type=jnp.float32).astype(jnp.bfloat16)
            xt[p, first:first + HALO] = part.reshape(HALO, batch, width)

    def turn_halo():
        @pl.when(tm > 0)
        def _():
            tail.wait_recv()
            turn(halo[...], 0)

        @pl.when(tm == 0)
        def _():
            xt[:, 0:HALO] = jnp.zeros((planes, HALO, batch, width), jnp.bfloat16)

    def unit(rank, pair, first):
        p = ranked(z, planes, rank)[0]
        lhs = xt[p, HALO - 1 - 2 * pair:HALO + window - 2 * pair].reshape((window + 1) * batch, width)
        part = jnp.dot(lhs, w[p, pair], preferred_element_type=jnp.float32)
        if first:
            acc[...] = part
        else:
            acc[...] += part

    def turn_own(i):
        if i == 0:
            load.wait()
        turn(xin[:, i * HALO:(i + 1) * HALO, :], HALO + i * HALO)

    work = [functools.partial(turn_own, i) for i in range(window // HALO)] + [turn_halo]
    for rank in range(planes):
        steps = [((rank, i, j), q) for i, j in flips for q in range(2) if (rank, i, j) != (0, 0, 0)]
        for n, (ranks, q) in enumerate(steps):
            process(ranks, q)
            for _ in range(-(-len(work) // (len(steps) - n))):
                if work:
                    work.pop(0)()
        while work:
            work.pop(0)()
        for ranks, q in steps:
            sibling_wait(tuple(ranked(me[d], sizes[d], ranks[d])[0] for d in (Z, A, B)), q)
        work = [functools.partial(unit, rank, pair, rank == 0 and pair == 0) for pair in range(pairs)]
    for item in work:
        item()

    total = (acc[batch:, :sensors] + acc[:window * batch, sensors:]).astype(jnp.bfloat16)
    for i in range(window // HALO):
        part = jnp.dot(to_batch, total[i * square:(i + 1) * square],
                       preferred_element_type=jnp.float32).astype(jnp.bfloat16)
        out_ref[:, i * HALO:(i + 1) * HALO, :] = part.reshape(batch, HALO, sensors)

    for cond, at, q, slot, device in sends:
        when(cond, lambda at=at, q=q, slot=slot, device=device: copy(at, q, slot, device).wait_send())
    pl.when(tm < n_tm - 1)(tail.wait_send)


def per_device(n_samp, n_tm, sources, operator, lag_order):
    batch, window, total_depth = sources.shape
    lags, depth, sensors = operator.shape
    side = math.isqrt(n_samp // 4)
    sizes = (n_samp // (side * side), side, side)
    width = side * side * depth
    return pl.pallas_call(
        functools.partial(fused, sizes, n_tm, lags),
        out_shape=jax.ShapeDtypeStruct((batch, window, sensors), jnp.bfloat16),
        in_specs=[
            pl.BlockSpec(memory_space=pl.ANY),
            pl.BlockSpec(memory_space=pltpu.VMEM),
            pl.BlockSpec(memory_space=pltpu.SMEM),
        ],
        out_specs=pl.BlockSpec(memory_space=pltpu.VMEM),
        scratch_shapes=[
            pltpu.VMEM((batch, window, total_depth), jnp.bfloat16),
            pltpu.VMEM((batch, HALO, total_depth), jnp.bfloat16),
            pltpu.VMEM((sizes[0], HALO + window, batch, width), jnp.bfloat16),
            pltpu.VMEM((sizes[0], lags // 2, width, 2 * sensors), jnp.bfloat16),
            pltpu.VMEM(((window + 1) * batch, 2 * sensors), jnp.float32),
            pltpu.SemaphoreType.DMA(()),
            pltpu.SemaphoreType.DMA(()),
            pltpu.SemaphoreType.DMA(()),
            pltpu.SemaphoreType.DMA((2, 7, n_samp)),
            pltpu.SemaphoreType.DMA((2, 2, n_samp)),
        ],
        compiler_params=pltpu.CompilerParams(
            collective_id=0, has_side_effects=True, vmem_limit_bytes=48 << 20),
    )(sources, operator, lag_order)


def solution(mesh):
    placed = (P("samp", "tm", None), P(None, "samp", None), P())
    return jax.shard_map(
        functools.partial(per_device, mesh.shape["samp"], mesh.shape["tm"]),
        mesh=mesh, in_specs=placed, out_specs=P("samp", "tm", None), check_vma=False,
    )
```

```python
import functools
import math

import jax
import jax.numpy as jnp
from jax import lax
from jax.experimental import pallas as pl
from jax.experimental.pallas import tpu as pltpu
from jax.sharding import PartitionSpec as P

MESH = pl.DeviceIdType.MESH
HALO = 16
Z, A, B = 0, 1, 2
ORDERS = ((Z, A, B),)
SHARES = ((0, 4),)
HOP = 3
POPS = 2
LAST = 11


def ranked(me, size, rank):
    if rank == 0:
        return me
    if size == 2:
        return 1 - me
    low = jnp.minimum(me, size - 1 - me)
    side = 1 - 2 * (me // ((size + 1) // 2))
    alternate = (rank + 1) // 2 if rank % 2 else -((rank + 1) // 2)
    near = rank <= 2 * low
    return me + side * jnp.where(near, alternate, rank - low)


def fused(sizes, n_tm, lags, src_hbm, op_ref, lag_ref, out_ref,
          xin, halo, xt, w, acc, in_sem, halo_send, halo_recv, send_sem, recv_sem):
    planes, side_size, _ = sizes
    batch, window, _ = xin.shape
    depth = op_ref.shape[1]
    sensors = op_ref.shape[2]
    pairs = lags // 2
    width = side_size * side_size * depth
    samp = lax.axis_index("samp")
    tm = lax.axis_index("tm")
    core = tm % 2
    sibling = tm + 1 - 2 * core
    z = samp // (side_size * side_size)
    y = (samp // side_size) % side_size
    x = samp % side_size
    stride_a = 1 + core * (side_size - 1)
    stride_b = side_size - core * (side_size - 1)
    me = (z, x + core * (y - x), y + core * (x - y))

    def flat(at):
        return at[Z] * (side_size * side_size) + at[A] * stride_a + at[B] * stride_b

    places = [[ranked(me[d], sizes[d], rank) for rank in range(sizes[d])] for d in (Z, A, B)]

    def peer(d, rank):
        at = list(me)
        at[d] = places[d][rank]
        return (flat(at), tm)

    load = pltpu.make_async_copy(src_hbm, xin, in_sem)
    load.start()

    barrier = pltpu.get_barrier_semaphore()
    expected = 1 + sum(sizes) - 3
    pl.semaphore_signal(barrier, inc=1, device_id=(samp, sibling), device_id_type=MESH)
    for d in (Z, A, B):
        for rank in range(1, sizes[d]):
            pl.semaphore_signal(barrier, inc=1, device_id=peer(d, rank), device_id_type=MESH)
    for cond, to in ((tm > 0, tm - 1), (tm < n_tm - 1, tm + 1)):
        pl.when(cond)(functools.partial(
            pl.semaphore_signal, barrier, inc=1, device_id=(samp, to), device_id_type=MESH))
        expected = expected + cond.astype(jnp.int32)

    own_rows = pl.multiple_of((samp % (side_size * side_size)) * depth, depth)
    for lag in range(lags):
        slot = jnp.int32(0)
        for k in range(lags):
            slot = jnp.where(lag_ref[k] == lag, k, slot)
        w[z, lag // 2, pl.ds(own_rows, depth), (lag % 2) * sensors:(lag % 2 + 1) * sensors] = op_ref[slot]

    pl.semaphore_wait(barrier, expected)

    def copy(ranks, q, of_core, slot, device):
        at = [places[d][ranks[d]] for d in (Z, A, B)]
        source = flat(at)
        rows = pl.multiple_of((source - at[Z] * (side_size * side_size)) * depth, depth)
        first, count = SHARES[q]
        half = pairs // 2
        ref = w.at[at[Z], pl.ds(of_core * half + half * first // 4, half * count // 4), pl.ds(rows, depth), :]
        return pltpu.make_async_remote_copy(
            src_ref=ref, dst_ref=ref,
            send_sem=send_sem.at[q, slot, source],
            recv_sem=recv_sem.at[1 if slot == 0 else 0, q, source],
            device_id=device, device_id_type=MESH)

    sends = []

    def send(cond, *args):
        if cond is None:
            copy(*args).start()
        else:
            pl.when(cond)(lambda: copy(*args).start())
        sends.append((cond, args))

    relayed = planes == 4
    inner = (z > 0) & (z < planes - 1)

    def process(ranks, q):
        order = ORDERS[q]
        last = -1
        for i, d in enumerate(order):
            if ranks[d]:
                last = i
        if last >= 0:
            copy(ranks, q, core, 1, (samp, sibling)).wait_recv()
        slot = 1
        for d in (A, B, Z):
            for rank in range(1, sizes[d]):
                far = relayed and d == Z and rank == planes - 1
                if d in order[last + 1:]:
                    send(inner if far else None, ranks, q, core, slot, peer(d, rank))
                elif far and last >= 0 and order[last] == Z and ranks[Z] == rank:
                    at = (planes - 1 - places[Z][rank], me[A], me[B])
                    send(inner, ranks, q, core, slot, (flat(at), tm))
                slot += 1
        if last >= 0:
            send(None, ranks, q, core, 0, (samp, sibling))

    def sibling_wait(ranks, q):
        copy(ranks, q, 1 - core, 0, (samp, sibling)).wait_recv()

    for q in range(len(ORDERS)):
        process((0, 0, 0), q)

    tail = pltpu.make_async_remote_copy(
        src_ref=src_hbm.at[:, pl.ds(window - HALO, HALO), :], dst_ref=halo,
        send_sem=halo_send, recv_sem=halo_recv,
        device_id=(samp, lax.rem(tm + 1, n_tm)), device_id_type=MESH)
    pl.when(tm < n_tm - 1)(tail.start)

    square = batch * HALO
    row = lax.broadcasted_iota(jnp.int32, (square, square), 0)
    col = lax.broadcasted_iota(jnp.int32, (square, square), 1)
    to_time = (col == (row % batch) * HALO + row // batch).astype(jnp.bfloat16)
    to_batch = (col == (row % HALO) * batch + row // HALO).astype(jnp.bfloat16)

    def turn(values, first):
        values = values.reshape(square, values.shape[-1])
        for p in range(planes):
            part = jnp.dot(to_time, values[:, p * width:(p + 1) * width],
                           preferred_element_type=jnp.float32).astype(jnp.bfloat16)
            xt[p, first:first + HALO] = part.reshape(HALO, batch, width)

    def turn_halo():
        @pl.when(tm > 0)
        def _():
            tail.wait_recv()
            turn(halo[...], 0)

        @pl.when(tm == 0)
        def _():
            xt[:, 0:HALO] = jnp.zeros((planes, HALO, batch, width), jnp.bfloat16)

    def turn_own(i):
        if i == 0:
            load.wait()
        turn(xin[:, i * HALO:(i + 1) * HALO, :], HALO + i * HALO)

    def unit(rank, pair, first):
        p = places[Z][rank]
        lhs = xt[p, HALO - 1 - 2 * pair:HALO + window - 2 * pair].reshape((window + 1) * batch, width)
        part = jnp.dot(lhs, w[p, pair], preferred_element_type=jnp.float32)
        if first:
            acc[...] = part
        else:
            acc[...] += part

    work = [functools.partial(turn_own, i) for i in range(window // HALO)] + [functools.partial(turn_halo)]
    steps = []
    for rank in range(planes):
        for i in range(side_size):
            for j in range(side_size):
                for q in range(len(ORDERS)):
                    if (rank, i, j) != (0, 0, 0):
                        hops = (i > 0) + (j > 0)
                        steps.append((rank + HOP * hops, q, rank, i, j))
    steps.sort()
    of_plane = {rank: [step for step in steps if step[2] == rank] for rank in range(planes)}
    for _, q, rank, i, j in steps:
        process((rank, i, j), q)
        for _ in range(POPS if not (i and j) else LAST):
            if work:
                work.pop(0)()
        if (q, rank, i, j) == of_plane[rank][-1][1:]:
            for _, q, rank, i, j in of_plane[rank]:
                work.append(functools.partial(sibling_wait, (rank, i, j), q))
            work.extend(functools.partial(unit, rank, pair, rank == 0 and pair == 0) for pair in range(pairs))
    for item in work:
        item()

    total = (acc[batch:, :sensors] + acc[:window * batch, sensors:]).astype(jnp.bfloat16)
    for i in range(window // HALO):
        part = jnp.dot(to_batch, total[i * square:(i + 1) * square],
                       preferred_element_type=jnp.float32).astype(jnp.bfloat16)
        out_ref[:, i * HALO:(i + 1) * HALO, :] = part.reshape(batch, HALO, sensors)

    for cond, args in sends:
        if cond is None:
            copy(*args).wait_send()
        else:
            pl.when(cond)(lambda args=args: copy(*args).wait_send())
    pl.when(tm < n_tm - 1)(tail.wait_send)


def per_device(n_samp, n_tm, sources, operator, lag_order):
    batch, window, total_depth = sources.shape
    lags, depth, sensors = operator.shape
    side = math.isqrt(n_samp // 4)
    sizes = (n_samp // (side * side), side, side)
    width = side * side * depth
    return pl.pallas_call(
        functools.partial(fused, sizes, n_tm, lags),
        out_shape=jax.ShapeDtypeStruct((batch, window, sensors), jnp.bfloat16),
        in_specs=[
            pl.BlockSpec(memory_space=pl.ANY),
            pl.BlockSpec(memory_space=pltpu.VMEM),
            pl.BlockSpec(memory_space=pltpu.SMEM),
        ],
        out_specs=pl.BlockSpec(memory_space=pltpu.VMEM),
        scratch_shapes=[
            pltpu.VMEM((batch, window, total_depth), jnp.bfloat16),
            pltpu.VMEM((batch, HALO, total_depth), jnp.bfloat16),
            pltpu.VMEM((sizes[0], HALO + window, batch, width), jnp.bfloat16),
            pltpu.VMEM((sizes[0], lags // 2, width, 2 * sensors), jnp.bfloat16),
            pltpu.VMEM(((window + 1) * batch, 2 * sensors), jnp.float32),
            pltpu.SemaphoreType.DMA(()),
            pltpu.SemaphoreType.DMA(()),
            pltpu.SemaphoreType.DMA(()),
            pltpu.SemaphoreType.DMA((len(ORDERS), sum(sizes) - 2, n_samp)),
            pltpu.SemaphoreType.DMA((2, len(ORDERS), n_samp)),
        ],
        compiler_params=pltpu.CompilerParams(
            collective_id=0, has_side_effects=True, vmem_limit_bytes=48 << 20),
    )(sources, operator, lag_order)


def solution(mesh):
    placed = (P("samp", "tm", None), P(None, "samp", None), P())
    return jax.shard_map(
        functools.partial(per_device, mesh.shape["samp"], mesh.shape["tm"]),
        mesh=mesh, in_specs=placed, out_specs=P("samp", "tm", None), check_vma=False,
    )
```

```python
import functools
import math

import jax
import jax.numpy as jnp
from jax import lax
from jax.experimental import pallas as pl
from jax.experimental.pallas import tpu as pltpu
from jax.sharding import PartitionSpec as P

MESH = pl.DeviceIdType.MESH
HALO = 16
GROUP = 4
Z, A, B = 0, 1, 2
ORDERS = ((Z, A, B),)
SHARES = ((0, 4),)
HOP = 3
POPS = 2
LAST = 11


def ranked(me, size, rank):
    if rank == 0:
        return me
    if size == 2:
        return 1 - me
    low = jnp.minimum(me, size - 1 - me)
    side = 1 - 2 * (me // ((size + 1) // 2))
    alternate = (rank + 1) // 2 if rank % 2 else -((rank + 1) // 2)
    near = rank <= 2 * low
    return me + side * jnp.where(near, alternate, rank - low)


def fused(sizes, n_tm, lags, src_hbm, op_ref, lag_ref, out_ref,
          xin, halo, xt, w, acc, in_sem, halo_send, halo_recv, send_sem, recv_sem):
    planes, side_size, _ = sizes
    batch, window, _ = xin.shape
    depth = op_ref.shape[1]
    sensors = op_ref.shape[2]
    pairs = lags // 2
    width = side_size * side_size * depth
    samp = lax.axis_index("samp")
    tm = lax.axis_index("tm")
    core = tm % 2
    sibling = tm + 1 - 2 * core
    z = samp // (side_size * side_size)
    y = (samp // side_size) % side_size
    x = samp % side_size
    stride_a = 1 + core * (side_size - 1)
    stride_b = side_size - core * (side_size - 1)
    me = (z, x + core * (y - x), y + core * (x - y))

    def flat(at):
        return at[Z] * (side_size * side_size) + at[A] * stride_a + at[B] * stride_b

    places = [[ranked(me[d], sizes[d], rank) for rank in range(sizes[d])] for d in (Z, A, B)]

    def peer(d, rank):
        at = list(me)
        at[d] = places[d][rank]
        return (flat(at), tm)

    load = pltpu.make_async_copy(src_hbm, xin, in_sem)
    load.start()

    barrier = pltpu.get_barrier_semaphore()
    expected = 1 + sum(sizes) - 3
    pl.semaphore_signal(barrier, inc=1, device_id=(samp, sibling), device_id_type=MESH)
    for d in (Z, A, B):
        for rank in range(1, sizes[d]):
            pl.semaphore_signal(barrier, inc=1, device_id=peer(d, rank), device_id_type=MESH)
    for cond, to in ((tm > 0, tm - 1), (tm < n_tm - 1, tm + 1)):
        pl.when(cond)(functools.partial(
            pl.semaphore_signal, barrier, inc=1, device_id=(samp, to), device_id_type=MESH))
        expected = expected + cond.astype(jnp.int32)

    own_rows = pl.multiple_of((samp % (side_size * side_size)) * depth, depth)
    for lag in range(lags):
        slot = jnp.int32(0)
        for k in range(lags):
            slot = jnp.where(lag_ref[k] == lag, k, slot)
        w[z, lag // 2, pl.ds(own_rows, depth), (lag % 2) * sensors:(lag % 2 + 1) * sensors] = op_ref[slot]

    pl.semaphore_wait(barrier, expected)

    def copy(ranks, q, of_core, slot, device):
        at = [places[d][ranks[d]] for d in (Z, A, B)]
        source = flat(at)
        rows = pl.multiple_of((source - at[Z] * (side_size * side_size)) * depth, depth)
        first, count = SHARES[q]
        half = pairs // 2
        ref = w.at[at[Z], pl.ds(of_core * half + half * first // 4, half * count // 4), pl.ds(rows, depth), :]
        return pltpu.make_async_remote_copy(
            src_ref=ref, dst_ref=ref,
            send_sem=send_sem.at[q, slot, source],
            recv_sem=recv_sem.at[1 if slot == 0 else 0, q, source],
            device_id=device, device_id_type=MESH)

    sends = []

    def send(cond, *args):
        if cond is None:
            copy(*args).start()
        else:
            pl.when(cond)(lambda: copy(*args).start())
        sends.append((cond, args))

    relayed = planes == 4
    inner = (z > 0) & (z < planes - 1)

    def process(ranks, q):
        order = ORDERS[q]
        last = -1
        for i, d in enumerate(order):
            if ranks[d]:
                last = i
        if last >= 0:
            copy(ranks, q, core, 1, (samp, sibling)).wait_recv()
        slot = 1
        for d in (A, B, Z):
            for rank in range(1, sizes[d]):
                far = relayed and d == Z and rank == planes - 1
                if d in order[last + 1:]:
                    send(inner if far else None, ranks, q, core, slot, peer(d, rank))
                elif far and last >= 0 and order[last] == Z and ranks[Z] == rank:
                    at = (planes - 1 - places[Z][rank], me[A], me[B])
                    send(inner, ranks, q, core, slot, (flat(at), tm))
                slot += 1
        if last >= 0:
            send(None, ranks, q, core, 0, (samp, sibling))

    def sibling_wait(ranks, q):
        copy(ranks, q, 1 - core, 0, (samp, sibling)).wait_recv()

    for q in range(len(ORDERS)):
        process((0, 0, 0), q)

    tail = pltpu.make_async_remote_copy(
        src_ref=src_hbm.at[:, pl.ds(window - HALO, HALO), :], dst_ref=halo,
        send_sem=halo_send, recv_sem=halo_recv,
        device_id=(samp, lax.rem(tm + 1, n_tm)), device_id_type=MESH)
    pl.when(tm < n_tm - 1)(tail.start)

    square = batch * HALO
    row = lax.broadcasted_iota(jnp.int32, (square, square), 0)
    col = lax.broadcasted_iota(jnp.int32, (square, square), 1)
    to_time = (col == (row % batch) * HALO + row // batch).astype(jnp.bfloat16)
    to_batch = (col == (row % HALO) * batch + row // HALO).astype(jnp.bfloat16)

    def turn(values, first):
        values = values.reshape(square, values.shape[-1])
        for p in range(planes):
            part = jnp.dot(to_time, values[:, p * width:(p + 1) * width],
                           preferred_element_type=jnp.float32).astype(jnp.bfloat16)
            xt[p, first:first + HALO] = part.reshape(HALO, batch, width)

    def turn_halo():
        @pl.when(tm > 0)
        def _():
            tail.wait_recv()
            turn(halo[...], 0)

        @pl.when(tm == 0)
        def _():
            xt[:, 0:HALO] = jnp.zeros((planes, HALO, batch, width), jnp.bfloat16)

    def turn_own(i):
        if i == 0:
            load.wait()
        turn(xin[:, i * HALO:(i + 1) * HALO, :], HALO + i * HALO)

    def unit(rank, pair, first):
        p = places[Z][rank]
        lhs = jnp.concatenate(
            [xt[p, HALO - 1 - 2 * k:HALO + window - 2 * k].reshape((window + 1) * batch, width)
             for k in range(pair, pair + GROUP)], axis=1)
        rhs = w[p, pair:pair + GROUP].reshape(GROUP * width, 2 * sensors)
        part = jnp.dot(lhs, rhs, preferred_element_type=jnp.float32)
        if first:
            acc[...] = part
        else:
            acc[...] += part

    work = [functools.partial(turn_own, i) for i in range(window // HALO)] + [functools.partial(turn_halo)]
    steps = []
    for rank in range(planes):
        for i in range(side_size):
            for j in range(side_size):
                for q in range(len(ORDERS)):
                    if (rank, i, j) != (0, 0, 0):
                        hops = (i > 0) + (j > 0)
                        steps.append((rank + HOP * hops, q, rank, i, j))
    steps.sort()
    of_plane = {rank: [step for step in steps if step[2] == rank] for rank in range(planes)}
    for _, q, rank, i, j in steps:
        process((rank, i, j), q)
        for _ in range(POPS if not (i and j) else LAST):
            if work:
                work.pop(0)()
        if (q, rank, i, j) == of_plane[rank][-1][1:]:
            for _, q, rank, i, j in of_plane[rank]:
                work.append(functools.partial(sibling_wait, (rank, i, j), q))
            work.extend(functools.partial(unit, rank, pair, rank == 0 and pair == 0) for pair in range(0, pairs, GROUP))
    for item in work:
        item()

    total = (acc[batch:, :sensors] + acc[:window * batch, sensors:]).astype(jnp.bfloat16)
    for i in range(window // HALO):
        part = jnp.dot(to_batch, total[i * square:(i + 1) * square],
                       preferred_element_type=jnp.float32).astype(jnp.bfloat16)
        out_ref[:, i * HALO:(i + 1) * HALO, :] = part.reshape(batch, HALO, sensors)

    for cond, args in sends:
        if cond is None:
            copy(*args).wait_send()
        else:
            pl.when(cond)(lambda args=args: copy(*args).wait_send())
    pl.when(tm < n_tm - 1)(tail.wait_send)


def per_device(n_samp, n_tm, sources, operator, lag_order):
    batch, window, total_depth = sources.shape
    lags, depth, sensors = operator.shape
    side = math.isqrt(n_samp // 4)
    sizes = (n_samp // (side * side), side, side)
    width = side * side * depth
    return pl.pallas_call(
        functools.partial(fused, sizes, n_tm, lags),
        out_shape=jax.ShapeDtypeStruct((batch, window, sensors), jnp.bfloat16),
        in_specs=[
            pl.BlockSpec(memory_space=pl.ANY),
            pl.BlockSpec(memory_space=pltpu.VMEM),
            pl.BlockSpec(memory_space=pltpu.SMEM),
        ],
        out_specs=pl.BlockSpec(memory_space=pltpu.VMEM),
        scratch_shapes=[
            pltpu.VMEM((batch, window, total_depth), jnp.bfloat16),
            pltpu.VMEM((batch, HALO, total_depth), jnp.bfloat16),
            pltpu.VMEM((sizes[0], HALO + window, batch, width), jnp.bfloat16),
            pltpu.VMEM((sizes[0], lags // 2, width, 2 * sensors), jnp.bfloat16),
            pltpu.VMEM(((window + 1) * batch, 2 * sensors), jnp.float32),
            pltpu.SemaphoreType.DMA(()),
            pltpu.SemaphoreType.DMA(()),
            pltpu.SemaphoreType.DMA(()),
            pltpu.SemaphoreType.DMA((len(ORDERS), sum(sizes) - 2, n_samp)),
            pltpu.SemaphoreType.DMA((2, len(ORDERS), n_samp)),
        ],
        compiler_params=pltpu.CompilerParams(
            collective_id=0, has_side_effects=True, vmem_limit_bytes=48 << 20),
    )(sources, operator, lag_order)


def solution(mesh):
    placed = (P("samp", "tm", None), P(None, "samp", None), P())
    return jax.shard_map(
        functools.partial(per_device, mesh.shape["samp"], mesh.shape["tm"]),
        mesh=mesh, in_specs=placed, out_specs=P("samp", "tm", None), check_vma=False,
    )
```
